32 devices in a mesh: tm: 2 (over x), cells: 16 (over z, y, core).
Axes of the slice: x: 2, y: 2, z: 4, core: 2. Of those that a mesh axis runs over, the one named last changes fastest.
Arguments:
- filtered: float32 [2, 8192], P('tm', 'cells'), may hold values from -6 to 6
- panels: bfloat16 [2, 8192, 512], P('tm', 'cells'), may hold values from -0.59662135 to 0.59662135
- tiles: bfloat16 [32, 9, 256, 256], P('cells'), may hold values from -0.06666667 to 1.0666667
- neighbours: int32 [32, 9], P('cells'), may hold values from 0 to 31, as said below
- noise_var: float32 [8192], P('cells'), may hold values from 0.5 to 8
- end_smoothed: float32 [8192], P('cells'), may hold values from -6 to 6
Outputs:
- smoothed: float32 [2, 8192], P('tm', 'cells')
The draws below stay inside these ranges and needn't reach their ends.
Inputs may be any that keep to these rules, and one draw needn't show every extreme that they name: `neighbours`: each block row b names 9 distinct block columns, b among them, all within the 10 consecutive blocks, counted cyclically over 32, that begin at block (b // 2 - 2) * 2.
All inputs are finite; a program needn't handle non-finite values.
Results may differ from the reference program's by a relative error of at most 0.00045.
Values may be sent and summed in bfloat16 or wider, within the bound.
A program may use at most 64 MiB of HBM per device.

```python
import math
import jax
import jax.numpy as jnp
from jax import lax

BLK = 256
R = 512
NBR = 9
BLK_DEV = 2
NB = 32
NC = 8192
STEPS = 2


def neighbour_pattern(key):
    pattern_key = jax.random.fold_in(key, 21)
    span_width = 5 * BLK_DEV
    row_numbers = jnp.arange(NB, dtype=jnp.int32)
    slots = jnp.arange(span_width, dtype=jnp.int32)
    scores = jax.random.randint(pattern_key, (NB, span_width), 0, 2 ** 20, dtype=jnp.int32) * span_width + slots[None, :]
    own_slot = 2 * BLK_DEV + row_numbers % BLK_DEV
    scores = jnp.where(slots[None, :] == own_slot[:, None], -1, scores)
    ranked = jnp.argsort(scores, axis=1, stable=True).astype(jnp.int32)
    offsets = ranked[:, :NBR]
    first_block = (row_numbers // BLK_DEV - 2) * BLK_DEV
    return jnp.mod(first_block[:, None] + offsets, NB).astype(jnp.int32)


def draw_neighbours(key, part):
    return neighbour_pattern(key)


def draw_tiles(key, part):
    pattern = neighbour_pattern(key)
    own_tile = (pattern == jnp.arange(NB, dtype=jnp.int32)[:, None]).astype(jnp.float32)
    spread = jax.random.normal(jax.random.fold_in(key, 22), (NB, NBR, BLK, BLK), jnp.float32)
    spread = jnp.clip(spread, -6.0, 6.0) * (0.5 / math.sqrt(NBR * BLK))
    unit_tile = jnp.eye(BLK, dtype=jnp.float32)
    result = spread + own_tile[:, :, None, None] * unit_tile[None, None]
    return result.astype(jnp.bfloat16)


def draw_panels(key, part):
    normalizer = 1.0 / (18.666666 * math.sqrt(R))
    left_ints = jax.random.randint(jax.random.fold_in(key, 1), (NC, R), -7, 8, dtype=jnp.int32).astype(jnp.float32)

    def one_step(step_key):
        right_ints = jax.random.randint(jax.random.fold_in(step_key, 2), (R, R), -7, 8, dtype=jnp.int32).astype(jnp.float32)
        fresh = jax.random.normal(jax.random.fold_in(step_key, 4), (NC, R), jnp.float32)
        mixed = jnp.dot(left_ints, right_ints, precision=lax.Precision.HIGHEST) * normalizer
        unit_value = 0.9 * mixed + 0.3 * fresh
        return jnp.clip(unit_value, -4.0, 4.0)
    step_keys = jax.random.split(jax.random.fold_in(key, 11), STEPS)
    unit_field = lax.map(one_step, step_keys)
    log_ten = math.log(10.0)
    row_draw = jax.random.uniform(jax.random.fold_in(key, 12), (1, NC, 1), jnp.float32)
    column_draw = jax.random.uniform(jax.random.fold_in(key, 13), (STEPS, 1, R), jnp.float32)
    row_scale = 0.3 * jnp.exp(row_draw * log_ten)
    column_scale = 0.2 * jnp.exp(column_draw * log_ten)
    result = 2.25 / math.sqrt(NC) * row_scale * column_scale * unit_field
    return result.astype(jnp.bfloat16)


def block_levels(rng, dims, cuts, least, high):
    loudness = 1.0
    for axis_at, parts in cuts:
        draws = jax.random.uniform(jax.random.fold_in(jax.random.fold_in(rng, 6), axis_at), (parts,), jnp.float32, least / len(cuts), high / len(cuts))
        loudness = loudness * jnp.repeat(jnp.exp(draws), dims[axis_at] // parts).reshape((-1,) + (1,) * (len(dims) - 1 - axis_at))
    return loudness


def noise(rng, dims, scale, bound, cuts=(), kind=jnp.bfloat16):
    loudness = block_levels(rng, dims, cuts, -0.22, 0.18) if cuts else 1.0
    array = jax.random.normal(rng, dims, jnp.float32) * scale * loudness
    return jnp.minimum(jnp.maximum(array, -bound), bound).astype(kind)


def setup_inputs(seed: int = 0) -> dict:
    splits = jax.random.split(jax.random.key(seed), 7)
    return {
        "filtered": noise(splits[0], (STEPS, NC), 1.0, 6.0, ((0, 2), (1, 16)), jnp.float32),
        "panels": draw_panels(jax.random.fold_in(splits[6], 71), 0),
        "tiles": draw_tiles(jax.random.fold_in(splits[6], 71), 0),
        "neighbours": draw_neighbours(jax.random.fold_in(splits[6], 71), 0),
        "noise_var": jnp.clip(jnp.exp(math.log(8.0) - 2.7725887 * jax.random.uniform(splits[4], (NC,), jnp.float32) ** block_levels(splits[4], (NC,), ((0, 16),), -0.2, 0.2)), 0.5, 8.0),
        "end_smoothed": noise(splits[5], (NC,), 1.0, 6.0, ((0, 16),), jnp.float32),
    }


def block_multiply(tiles, neighbours, field):
    block_count = tiles.shape[0]
    blocks = field.reshape(block_count, BLK, -1).astype(jnp.float32)
    total = jnp.zeros(blocks.shape, jnp.float32)
    for column in range(NBR):
        picked = blocks[neighbours[:, column]]
        total = total + jnp.einsum('bij,bjc->bic', tiles[:, column].astype(jnp.float32), picked, precision=lax.Precision.HIGHEST)
    return total.reshape(field.shape)

def cholesky_apply(factor, right_side):
    column = right_side[:, None]
    halfway = lax.linalg.triangular_solve(factor, column, left_side=True, lower=True)
    solved = lax.linalg.triangular_solve(factor, halfway, left_side=True, lower=True, transpose_a=True)
    return solved[:, 0]

def reference(filtered, panels, tiles, neighbours, noise_var, end_smoothed):
    maximal_precision = lax.Precision.HIGHEST

    def backward(subsequent_value, inputs):
        state_mean, panel = inputs
        advected = block_multiply(tiles, neighbours, panel)
        rescaled_rows = advected / noise_var[:, None]
        system = jnp.eye(R, dtype=jnp.float32) + jnp.dot(advected.T, rescaled_rows, precision=maximal_precision)
        factor = jnp.linalg.cholesky(system)
        predicted_state = block_multiply(tiles, neighbours, state_mean.astype(jnp.bfloat16)[:, None])[:, 0]
        rank_projected = jnp.dot(subsequent_value - predicted_state, rescaled_rows, precision=maximal_precision)
        coefficient = cholesky_apply(factor, rank_projected)
        result = state_mean + jnp.dot(panel.astype(jnp.float32), coefficient, precision=maximal_precision)
        return (result, result)
    carried, smoothed = lax.scan(backward, end_smoothed, (filtered, panels), reverse=True)
    return smoothed
```

```python
import functools
import jax
import jax.numpy as jnp
from jax import lax
from jax.experimental import pallas as pl
from jax.experimental.pallas import tpu as pltpu
from jax.sharding import PartitionSpec as P

HI = lax.Precision.HIGHEST
B = 128
MESH = pl.DeviceIdType.MESH
PLAN = ("D0 D1 R0 F0", "D2 X0 R1 F1", "X1 S0 D3 R2", "F2 X2 A0 S1", "R3 F3 X3 V0", "A1 S2 V1 S3", "A2 V2 A3 V3")


def invert_block(s, n, hooks=()):
    groups = n // 8
    hooks = list(hooks)
    rows = [s[8 * g : 8 * g + 8, :] for g in range(groups)]
    lane = lax.broadcasted_iota(jnp.int32, (8, n), 1)
    sub = lax.broadcasted_iota(jnp.int32, (8, n), 0)
    spread = lambda v, j: jnp.broadcast_to(v[j : j + 1, :], (8, n))
    pending = []
    for g in range(groups):
        k = 8 * g
        inside = (lane >= k) & (lane < k + 8)
        col = lambda i, j, k=k: jnp.broadcast_to(rows[i][:, k + j : k + j + 1], (8, n))
        d = [col(g, j) for j in range(8)]
        lead = jnp.where(inside, jnp.where(lane - k == sub, 1.0, 0.0), rows[g])
        each = -(-len(pending) // 8)
        for j in range(8):
            inverse = 1.0 / spread(d[j], j)
            for l in range(j + 1, 8):
                moved = spread(d[l], j) * inverse
                d[l] = jnp.where(sub == j, moved, d[l] - d[j] * moved)
            fresh = spread(lead, j) * inverse
            lead = jnp.where(sub == j, fresh, lead - d[j] * fresh)
            for _ in range(each):
                if pending:
                    pending.pop(0)()
        spreads = [spread(lead, j) for j in range(8)]

        def update(i, spreads=spreads, inside=inside, col=col):
            cols = [col(i, j) for j in range(8)]
            a = jnp.where(inside, 0.0, rows[i])
            b = cols[4] * spreads[4]
            for j in range(4):
                a = a - cols[j] * spreads[j]
            for j in range(5, 8):
                b = b + cols[j] * spreads[j]
            rows[i] = a - b

        rows[g] = lead
        if g + 1 < groups:
            update(g + 1)
        pending = [functools.partial(update, i) for i in list(range(g + 2, groups)) + list(range(g))]
        if hooks:
            hooks.pop(0)()
    for run in pending + hooks:
        run()
    return jnp.concatenate(rows, axis=0)


def dot(a, b):
    return jnp.dot(a, b, precision=HI, preferred_element_type=jnp.float32)


def dot_t(a, b):
    return lax.dot_general(a, b, (((1,), (1,)), ((), ())), precision=HI, preferred_element_type=jnp.float32)


def split3(v):
    a = v.astype(jnp.bfloat16)
    rest = v - a.astype(jnp.float32)
    b = rest.astype(jnp.bfloat16)
    c = (rest - b.astype(jnp.float32)).astype(jnp.bfloat16)
    return a, b, c


def kernel(n, sections, pan_ref, filt_ref, tiles_ref, near_ref, noise_ref, end_ref, out_ref, adv, scaled, window, means, tiles,
           dense, divisor, q_ref, t_ref, u_ref, linv, later, mine, seen, passed, sem_tiles, sem_halo, sem_mean, sem_sum, sem_share,
           sem_tm, *sums):
    me = lax.axis_index("cells")
    section = lax.axis_index("tm")
    cells, rank = adv.shape
    blocks, per_row, size = tiles.shape[:3]
    chunks = rank // B
    packed, landed, parts, slots, full = (sums[i * chunks : (i + 1) * chunks] for i in range(5))
    chips = n // 2
    per = B // n
    chip, core = me // 2, me % 2
    odd = chip % 2
    partner = chip * 2 + (1 - core)
    has_next = section < sections - 1
    has_before = section > 0
    is_last = section == sections - 1

    fetch = pltpu.make_async_copy(tiles_ref, tiles, sem_tiles)
    fetch.start()
    barrier = pltpu.get_barrier_semaphore()
    for k in range(1, n):
        pl.semaphore_signal(barrier, inc=1, device_id={"cells": (me + k) % n}, device_id_type=MESH)

    @pl.when(has_next)
    def _():
        pl.semaphore_signal(barrier, inc=1, device_id={"tm": section + 1}, device_id_type=MESH)

    @pl.when(has_before)
    def _():
        pl.semaphore_signal(barrier, inc=1, device_id={"tm": section - 1}, device_id_type=MESH)

    pl.semaphore_wait(barrier, n - 1 + has_next.astype(jnp.int32) + has_before.astype(jnp.int32))

    def remote(source, target, send, receive, cell):
        return pltpu.make_async_remote_copy(source, target, send, receive, device_id={"cells": cell}, device_id_type=MESH)

    def arrive(ref, sem):
        pltpu.make_async_copy(ref, ref, sem).wait()

    def mean_copy(offset):
        return remote(filt_ref, means.at[2 - offset], sem_mean.at[0, 2 - offset], sem_mean.at[1, 2 - offset], (me + offset + n) % n)

    def own_chunk(j):
        return pan_ref.at[0, :, j * B : (j + 1) * B]

    def near(j):
        return remote(own_chunk(j), window.at[1 + 2 * core, j], sem_halo.at[0, 0, j], sem_halo.at[1, 0, j], partner)

    def direct(j):
        return remote(own_chunk(j), window.at[4 * odd, j], sem_halo.at[0, 1, j], sem_halo.at[1, 1, j], me + 2 - 4 * odd)

    def relay(j):
        return remote(
            window.at[4 - 4 * odd, j], window.at[4 * odd, j], sem_halo.at[0, 2, j], sem_halo.at[1, 2, j],
            (me + 4 - 8 * odd + n) % n,
        )

    def forward(j):
        return remote(window.at[4 - 4 * core, j], window.at[3 - 2 * core, j], sem_halo.at[0, 3, j], sem_halo.at[1, 3, j], partner)

    for j in range(chunks):
        direct(j).start()
        near(j).start()
        if j == 0:
            for offset in (1, -1, 2, -2):
                mean_copy(offset).start()

    divisor[...] = jnp.broadcast_to(noise_ref[...], (B, cells)).T
    fetch.wait()
    first_block = (me - 2) * blocks
    total_blocks = n * blocks
    for b in range(blocks):
        places = [(near_ref[b, k] - first_block + total_blocks) % total_blocks for k in range(per_row)]
        for w in range(5 * blocks):
            at = jnp.int32(0)
            found = jnp.int32(0)
            for k in range(per_row):
                hit = (places[k] == w).astype(jnp.int32)
                at = jnp.maximum(at, hit * k)
                found = jnp.maximum(found, hit)
            keep = jnp.full((size, size), found, jnp.int32) > 0
            tile = tiles[b, at].astype(jnp.float32)
            dense[b * size : (b + 1) * size, w * size : (w + 1) * size] = jnp.where(keep, tile, 0.0).astype(jnp.bfloat16)

    for offset in (1, -1, 2, -2):
        mean_copy(offset).wait()
    pred = jnp.zeros((1, cells), jnp.float32)
    for s in range(5):
        row = filt_ref[...] if s == 2 else means[s]
        pred = pred + lax.dot_general(
            row.astype(jnp.bfloat16), dense[:, s * cells : (s + 1) * cells],
            (((1,), (1,)), ((), ())), preferred_element_type=jnp.float32,
        )

    def exchange(j):
        return remote(packed[j].at[1 - core], landed[j], sem_sum.at[j, 0], sem_sum.at[j, 1], partner)

    def spread(j, k):
        q = (chip + k) % chips
        return remote(parts[j].at[q], slots[j].at[k], sem_sum.at[j, 2], sem_sum.at[j, 3], q * 2 + core)

    def collect(j, k):
        q = (chip + k) % chips
        piece = full[j].at[core, chip]
        return remote(piece, piece, sem_sum.at[j, 4], sem_sum.at[j, 5], q * 2 + core)

    def across(j):
        return remote(full[j].at[core], full[j].at[core], sem_sum.at[j, 6], sem_sum.at[j, 7], partner)

    def project():
        gap = (later[...] - pred)
        mine[...] = dot(gap, scaled[...])
        for k in range(1, n):
            remote(mine, seen.at[me], sem_share.at[0], sem_share.at[1], (me + k) % n).start()
        seen[me] = mine[...]

    def shared():
        arrive(seen.at[1:], sem_share.at[1])
        total = seen[0]
        for k in range(1, n):
            total = total + seen[k]
        return total

    def event_d(j):
        direct(j).wait_recv()
        relay(j).start()

        @pl.when(core == odd)
        def _():
            forward(j).start()

    def event_r(j):
        relay(j).wait_recv()

        @pl.when(core != odd)
        def _():
            forward(j).start()

    def event_f(j):
        here = slice(j * B, (j + 1) * B)
        near(j).wait_recv()
        forward(j).wait_recv()
        product = jnp.zeros((cells, B), jnp.float32)
        for s in range(5):
            piece = pan_ref[0, :, here] if s == 2 else window[s, j]
            product = product + jnp.dot(dense[:, s * cells : (s + 1) * cells], piece, preferred_element_type=jnp.float32)
        adv[:, here] = product
        scaled[:, here] = product / divisor[...]
        value = lax.dot_general(
            scaled[:, here], adv[:, : (j + 1) * B], (((0,), (0,)), ((), ())), precision=HI, preferred_element_type=jnp.float32
        )
        for half in range(2):
            for q in range(chips):
                at = (half * chips + q) * per
                packed[j][half, q] = value[at : at + per]
        exchange(j).start()
        if j == chunks - 1:

            @pl.when(is_last)
            def _():
                later[...] = end_ref[...]
                project()

    def event_x(j):
        exchange(j).wait_recv()
        parts[j][...] = packed[j][core] + landed[j][...]
        for k in range(1, chips):
            spread(j, k).start()

    def event_s(j):
        arrive(slots[j].at[1:], sem_sum.at[j, 3])
        total = parts[j][chip]
        for k in range(1, chips):
            total = total + slots[j][k]
        full[j][core, chip] = total
        for k in range(1, chips):
            collect(j, k).start()

    def event_a(j):
        arrive(full[j].at[core, 1:], sem_sum.at[j, 5])
        across(j).start()

    eye = jnp.where(lax.broadcasted_iota(jnp.int32, (B, B), 0) == lax.broadcasted_iota(jnp.int32, (B, B), 1), 1.0, 0.0)

    def event_v(j):
        across(j).wait_recv()
        row = full[j][...].reshape(B, (j + 1) * B)
        for i in range(j):
            here = slice(i * B, (i + 1) * B)
            u = row[:, here]
            if i > 0:
                u = u - dot_t(t_ref[j, :, : i * B], u_ref[i, :, : i * B])
            u_ref[j, :, here] = u
            t_ref[j, :, here] = dot(u, q_ref[i])
        schur = row[:, j * B :] + eye
        if j > 0:
            schur = schur - dot_t(t_ref[j, :, : j * B], u_ref[j, :, : j * B])
        linv[j * B : (j + 1) * B, j * B : (j + 1) * B] = eye
        if j + 1 < chunks:
            linv[j * B : (j + 1) * B, (j + 1) * B :] = jnp.zeros((B, rank - (j + 1) * B), jnp.float32)
        if j > 0:
            linv[j * B : (j + 1) * B, : j * B] = -dot(t_ref[j, :, : j * B], linv[: j * B, : j * B])
        q_ref[j] = invert_block(schur, B)

    events = {"D": event_d, "R": event_r, "F": event_f, "X": event_x, "S": event_s, "A": event_a, "V": event_v}
    for name in " ".join(PLAN).split():
        events[name[0]](int(name[1:]))


    def handoff():
        return pltpu.make_async_remote_copy(
            later, passed, sem_tm.at[0], sem_tm.at[1], device_id={"tm": section - 1}, device_id_type=MESH
        )

    @pl.when(has_next)
    def _():
        handoff().wait_recv()
        later[...] = passed[...]
        project()

    g = shared()
    arrive(seen.at[1:], sem_share.at[0])
    y = dot_t(g, linv[...])
    z = jnp.concatenate([dot(y[:, j * B : (j + 1) * B], q_ref[j]) for j in range(chunks)], axis=1)
    coefficient = dot(z, linv[...])
    moved = sum(
        lax.dot_general(c, pan_ref[0], (((1,), (1,)), ((), ())), preferred_element_type=jnp.float32) for c in split3(coefficient)
    )
    result = filt_ref[...] + moved
    out_ref[...] = result

    @pl.when(has_before)
    def _():
        later[...] = result
        handoff().start()

    for j in range(chunks):
        for copy in (near(j), direct(j), relay(j), forward(j), exchange(j), across(j)):
            copy.wait_send()
        arrive(parts[j].at[1:], sem_sum.at[j, 2])
        arrive(full[j].at[core, 1:], sem_sum.at[j, 4])

    @pl.when(has_before)
    def _():
        handoff().wait_send()


def smooth(filtered, panels, tiles, neighbours, noise_var, end_smoothed):
    n, sections = lax.axis_size("cells"), lax.axis_size("tm")
    steps, cells, rank = panels.shape
    assert steps == 1 and n % 4 == 0 and B % n == 0
    chunks, chips, per = rank // B, n // 2, B // n
    f32 = jnp.float32
    vmem = pl.BlockSpec(memory_space=pltpu.VMEM)

    def sums(*lead):
        return [pltpu.VMEM((*lead, chips, per, (j + 1) * B), f32) for j in range(chunks)]

    return pl.pallas_call(
        functools.partial(kernel, n, sections),
        out_shape=jax.ShapeDtypeStruct((steps, cells), f32),
        in_specs=[vmem, vmem, pl.BlockSpec(memory_space=pl.ANY), pl.BlockSpec(memory_space=pltpu.SMEM), vmem, vmem],
        out_specs=vmem,
        scratch_shapes=[
            pltpu.VMEM((cells, rank), f32),
            pltpu.VMEM((cells, rank), f32),
            pltpu.VMEM((5, chunks, cells, B), panels.dtype),
            pltpu.VMEM((5, steps, cells), f32),
            pltpu.VMEM(tiles.shape, tiles.dtype),
            pltpu.VMEM((cells, 5 * cells), tiles.dtype),
            pltpu.VMEM((cells, B), f32),
            pltpu.VMEM((chunks, B, B), f32),
            pltpu.VMEM((chunks, B, rank), f32),
            pltpu.VMEM((chunks, B, rank), f32),
            pltpu.VMEM((rank, rank), f32),
            pltpu.VMEM((1, cells), f32),
            pltpu.VMEM((1, rank), f32),
            pltpu.VMEM((n, 1, rank), f32),
            pltpu.VMEM((1, cells), f32),
            pltpu.SemaphoreType.DMA,
            pltpu.SemaphoreType.DMA((2, 4, chunks)),
            pltpu.SemaphoreType.DMA((2, 5)),
            pltpu.SemaphoreType.DMA((chunks, 8)),
            pltpu.SemaphoreType.DMA((2,)),
            pltpu.SemaphoreType.DMA((2,)),
            *sums(2), *sums(), *sums(), *sums(), *sums(2),
        ],
        compiler_params=pltpu.CompilerParams(collective_id=0, has_side_effects=True, vmem_limit_bytes=56 << 20),
    )(panels, filtered, tiles, neighbours, noise_var[None], end_smoothed[None])


def solution(mesh):
    placed = (
        P("tm", "cells"),
        P("tm", "cells", None),
        P("cells", None, None, None),
        P("cells", None),
        P("cells"),
        P("cells"),
    )
    return jax.shard_map(smooth, mesh=mesh, in_specs=placed, out_specs=P("tm", "cells"), check_vma=False)
```

```python
import functools
import jax
import jax.numpy as jnp
from jax import lax
from jax.experimental import pallas as pl
from jax.experimental.pallas import tpu as pltpu
from jax.sharding import PartitionSpec as P

HI = lax.Precision.HIGHEST
B = 128
MESH = pl.DeviceIdType.MESH
PLAN = ("B0 D0 B1 D1", "P0 R0 F0 D2", "R1 X0 F1 D3", "R2 X1 S0 F2", "R3 X2 S1 F3", "A0 A1 S2 X3", "W0 V0 W1 A2", "S3 V1 W2 A3", "V2 W3 V3")
INSIDE = {0: {}, 1: {}, 2: {1: "L1"}, 3: {1: "L2", 4: "L3"}}


def invert_block(s, n, inside_of=None):
    groups = n // 8
    inside_of = inside_of or {}
    rows = [s[8 * g : 8 * g + 8, :] for g in range(groups)]
    lane = lax.broadcasted_iota(jnp.int32, (8, n), 1)
    sub = lax.broadcasted_iota(jnp.int32, (8, n), 0)
    spread = lambda v, j: jnp.broadcast_to(v[j : j + 1, :], (8, n))
    pending = []
    for g in range(groups):
        k = 8 * g
        inside = (lane >= k) & (lane < k + 8)
        col = lambda i, j, k=k: jnp.broadcast_to(rows[i][:, k + j : k + j + 1], (8, n))
        d = [col(g, j) for j in range(8)]
        lead = jnp.where(inside, jnp.where(lane - k == sub, 1.0, 0.0), rows[g])
        each = -(-len(pending) // 8)
        for j in range(8):
            inverse = 1.0 / spread(d[j], j)
            for l in range(j + 1, 8):
                moved = spread(d[l], j) * inverse
                d[l] = jnp.where(sub == j, moved, d[l] - d[j] * moved)
            fresh = spread(lead, j) * inverse
            lead = jnp.where(sub == j, fresh, lead - d[j] * fresh)
            for _ in range(each):
                if pending:
                    pending.pop(0)()
        spreads = [spread(lead, j) for j in range(8)]

        def update(i, spreads=spreads, inside=inside, col=col):
            cols = [col(i, j) for j in range(8)]
            a = jnp.where(inside, 0.0, rows[i])
            b = cols[4] * spreads[4]
            for j in range(4):
                a = a - cols[j] * spreads[j]
            for j in range(5, 8):
                b = b + cols[j] * spreads[j]
            rows[i] = a - b

        rows[g] = lead
        if g + 1 < groups:
            update(g + 1)
        pending = [functools.partial(update, i) for i in list(range(g + 2, groups)) + list(range(g))]
        if g in inside_of:
            inside_of[g]()
    for run in pending:
        run()
    return jnp.concatenate(rows, axis=0)


def dot(a, b):
    return jnp.dot(a, b, precision=HI, preferred_element_type=jnp.float32)


def dot_t(a, b):
    return lax.dot_general(a, b, (((1,), (1,)), ((), ())), precision=HI, preferred_element_type=jnp.float32)


def down(v, ref):
    length, width = ref.shape
    spread = jnp.broadcast_to(v, (B, length))
    column = jnp.concatenate([spread[:, i : i + B].T for i in range(0, length, B)], axis=0)
    return jnp.sum(ref[...] * jnp.concatenate([column] * (width // B), axis=1), axis=0, keepdims=True)


def lanes(t):
    folded = t[:, :B]
    for i in range(B, t.shape[1], B):
        folded = folded + t[:, i : i + B]
    sums = [jnp.sum(folded[i : i + B].T, axis=0, keepdims=True) for i in range(0, t.shape[0], B)]
    return jnp.concatenate(sums, axis=1)


def split3(v):
    a = v.astype(jnp.bfloat16)
    rest = v - a.astype(jnp.float32)
    b = rest.astype(jnp.bfloat16)
    c = (rest - b.astype(jnp.float32)).astype(jnp.bfloat16)
    return a, b, c


def kernel(n, sections, pan_ref, filt_ref, tiles_ref, near_ref, noise_ref, end_ref, out_ref, adv, scaled, window, means, tiles,
           dense, divisor, q_ref, t_ref, u_ref, linv, pred, later, mine, seen, passed, sem_tiles, sem_halo, sem_mean, sem_sum, sem_share,
           sem_tm, *sums):
    me = lax.axis_index("cells")
    section = lax.axis_index("tm")
    cells, rank = adv.shape
    blocks, per_row, size = tiles.shape[:3]
    chunks = rank // B
    spans = spans_of(chunks)
    packed, landed, parts, slots, full = (sums[i * len(spans) : (i + 1) * len(spans)] for i in range(5))
    chips = n // 2
    chip, core = me // 2, me % 2
    odd = chip % 2
    partner = chip * 2 + (1 - core)
    has_next = section < sections - 1
    has_before = section > 0
    is_last = section == sections - 1

    fetch = pltpu.make_async_copy(tiles_ref, tiles, sem_tiles)
    fetch.start()
    barrier = pltpu.get_barrier_semaphore()
    for k in range(1, n):
        pl.semaphore_signal(barrier, inc=1, device_id={"cells": (me + k) % n}, device_id_type=MESH)

    @pl.when(has_next)
    def _():
        pl.semaphore_signal(barrier, inc=1, device_id={"tm": section + 1}, device_id_type=MESH)

    @pl.when(has_before)
    def _():
        pl.semaphore_signal(barrier, inc=1, device_id={"tm": section - 1}, device_id_type=MESH)

    pl.semaphore_wait(barrier, n - 1 + has_next.astype(jnp.int32) + has_before.astype(jnp.int32))

    def remote(source, target, send, receive, cell):
        return pltpu.make_async_remote_copy(source, target, send, receive, device_id={"cells": cell}, device_id_type=MESH)

    def arrive(ref, sem):
        pltpu.make_async_copy(ref, ref, sem).wait()

    def mean_copy(offset):
        return remote(filt_ref, means.at[2 - offset], sem_mean.at[0, 2 - offset], sem_mean.at[1, 2 - offset], (me + offset + n) % n)

    def own_chunk(j):
        return pan_ref.at[0, :, j * B : (j + 1) * B]

    def near(j):
        return remote(own_chunk(j), window.at[1 + 2 * core, j], sem_halo.at[0, 0, j], sem_halo.at[1, 0, j], partner)

    def direct(j):
        return remote(own_chunk(j), window.at[4 * odd, j], sem_halo.at[0, 1, j], sem_halo.at[1, 1, j], me + 2 - 4 * odd)

    def relay(j):
        return remote(
            window.at[4 - 4 * odd, j], window.at[4 * odd, j], sem_halo.at[0, 2, j], sem_halo.at[1, 2, j],
            (me + 4 - 8 * odd + n) % n,
        )

    def forward(j):
        return remote(window.at[4 - 4 * core, j], window.at[3 - 2 * core, j], sem_halo.at[0, 3, j], sem_halo.at[1, 3, j], partner)

    for j in range(chunks):
        direct(j).start()
        near(j).start()
        if j == 0:
            for offset in (1, -1, 2, -2):
                mean_copy(offset).start()

    divisor[...] = jnp.broadcast_to(noise_ref[...], (B, cells)).T
    first_block = (me - 2) * blocks
    total_blocks = n * blocks

    def event_b(b):
        if b == 0:
            fetch.wait()
        places = [(near_ref[b, k] - first_block + total_blocks) % total_blocks for k in range(per_row)]
        for w in range(5 * blocks):
            at = jnp.int32(0)
            found = jnp.int32(0)
            for k in range(per_row):
                hit = (places[k] == w).astype(jnp.int32)
                at = jnp.maximum(at, hit * k)
                found = jnp.maximum(found, hit)
            keep = jnp.full((size, size), found, jnp.int32) > 0
            tile = tiles[b, at].astype(jnp.float32)
            dense[b * size : (b + 1) * size, w * size : (w + 1) * size] = jnp.where(keep, tile, 0.0).astype(jnp.bfloat16)

    def event_p(_):
        for offset in (1, -1, 2, -2):
            mean_copy(offset).wait()
        total = jnp.zeros((1, cells), jnp.float32)
        for s in range(5):
            row = filt_ref[...] if s == 2 else means[s]
            total = total + lax.dot_general(
                row.astype(jnp.bfloat16), dense[:, s * cells : (s + 1) * cells],
                (((1,), (1,)), ((), ())), preferred_element_type=jnp.float32,
            )
        pred[...] = total

    def exchange(j):
        return remote(packed[j].at[1 - core], landed[j], sem_sum.at[j, 0], sem_sum.at[j, 1], partner)

    def spread(j, k):
        q = (chip + k) % chips
        return remote(parts[j].at[q], slots[j].at[k], sem_sum.at[j, 2], sem_sum.at[j, 3], q * 2 + core)

    def collect(j, k):
        q = (chip + k) % chips
        piece = full[j].at[core, chip]
        return remote(piece, piece, sem_sum.at[j, 4], sem_sum.at[j, 5], q * 2 + core)

    def across(j):
        return remote(full[j].at[core], full[j].at[core], sem_sum.at[j, 6], sem_sum.at[j, 7], partner)

    def project():
        gap = later[...] - pred[...]
        mine[...] = down(gap, scaled)
        for k in range(1, n):
            remote(mine, seen.at[me], sem_share.at[0], sem_share.at[1], (me + k) % n).start()
        seen[me] = mine[...]

    def shared():
        arrive(seen.at[1:], sem_share.at[1])
        total = seen[0]
        for k in range(1, n):
            total = total + seen[k]
        return total

    def event_d(j):
        direct(j).wait_recv()
        relay(j).start()

        @pl.when(core == odd)
        def _():
            forward(j).start()

    def event_r(j):
        relay(j).wait_recv()

        @pl.when(core != odd)
        def _():
            forward(j).start()

    def event_f(g):
        first, end = spans[g]
        here = slice(first * B, end * B)
        for j in range(first, end):
            near(j).wait_recv()
            forward(j).wait_recv()
        product = jnp.zeros((cells, (end - first) * B), jnp.float32)
        for s in range(5):
            if s == 2:
                piece = pan_ref[0, :, here]
            else:
                piece = jnp.concatenate([window[s, j] for j in range(first, end)], axis=1)
            product = product + jnp.dot(dense[:, s * cells : (s + 1) * cells], piece, preferred_element_type=jnp.float32)
        adv[:, here] = product
        scaled[:, here] = product / jnp.concatenate([divisor[...]] * (end - first), axis=1)
        value = lax.dot_general(
            scaled[:, here], adv[:, : end * B], (((0,), (0,)), ((), ())), precision=HI, preferred_element_type=jnp.float32
        )
        per = (end - first) * B // n
        for half in range(2):
            for q in range(chips):
                at = (half * chips + q) * per
                packed[g][half, q] = value[at : at + per]
        exchange(g).start()
        if end == chunks:

            @pl.when(is_last)
            def _():
                later[...] = end_ref[...]
                project()

    def event_x(j):
        exchange(j).wait_recv()
        parts[j][...] = packed[j][core] + landed[j][...]
        for k in range(1, chips):
            spread(j, k).start()

    def event_s(j):
        arrive(slots[j].at[1:], sem_sum.at[j, 3])
        total = parts[j][chip]
        for k in range(1, chips):
            total = total + slots[j][k]
        full[j][core, chip] = total
        for k in range(1, chips):
            collect(j, k).start()

    def event_a(j):
        arrive(full[j].at[core, 1:], sem_sum.at[j, 5])
        across(j).start()

    eye = jnp.where(lax.broadcasted_iota(jnp.int32, (B, B), 0) == lax.broadcasted_iota(jnp.int32, (B, B), 1), 1.0, 0.0)

    def event_w(g):
        across(g).wait_recv()

    def block(j, i):
        g = max(at for at, span in enumerate(spans) if span[0] <= j)
        first, end = spans[g]
        value = full[g][:, :, :, i * B : (i + 1) * B].reshape((end - first) * B, B)
        return value[(j - first) * B : (j - first + 1) * B]

    def upper(j, i):
        u = block(j, i)
        if i > 0:
            u = u - dot_t(t_ref[j, :, : i * B], u_ref[i, :, : i * B])
        u_ref[j, :, i * B : (i + 1) * B] = u

    def times_inverse(j, i):
        here = slice(i * B, (i + 1) * B)
        t_ref[j, :, here] = dot(u_ref[j, :, here], q_ref[i * B : (i + 1) * B, :])

    def event_l(j):
        linv[j * B : (j + 1) * B, : j * B] = -dot(t_ref[j, :, : j * B], linv[: j * B, : j * B])

    def event_u(j):
        for i in range(j - 1):
            upper(j, i)
            times_inverse(j, i)
        upper(j, j - 1)
        ready.add(j)

    ready = set()

    def event_v(j):
        if j > 0 and j not in ready:
            event_u(j)
        if j > 0:
            times_inverse(j, j - 1)
        schur = block(j, j) + eye
        if j > 0:
            schur = schur - dot_t(t_ref[j, :, : j * B], u_ref[j, :, : j * B])
        linv[j * B : (j + 1) * B, j * B : (j + 1) * B] = eye
        if j + 1 < chunks:
            linv[j * B : (j + 1) * B, (j + 1) * B :] = jnp.zeros((B, rank - (j + 1) * B), jnp.float32)
        q_ref[j * B : (j + 1) * B, :] = invert_block(
            schur, B, {group: functools.partial(play, names) for group, names in INSIDE[j].items()}
        )

    events = {
        "B": event_b, "P": event_p, "D": event_d, "R": event_r, "F": event_f, "X": event_x, "S": event_s,
        "A": event_a, "W": event_w, "U": event_u, "L": event_l, "V": event_v,
    }

    def play(names):
        for name in names.split():
            events[name[0]](int(name[1:]))

    for names in PLAN:
        play(names)

    def handoff():
        return pltpu.make_async_remote_copy(
            later, passed, sem_tm.at[0], sem_tm.at[1], device_id={"tm": section - 1}, device_id_type=MESH
        )

    @pl.when(has_next)
    def _():
        handoff().wait_recv()
        later[...] = passed[...]
        project()

    g = shared()
    arrive(seen.at[1:], sem_share.at[0])
    y = lanes(linv[...] * g)
    z = lanes(q_ref[...] * jnp.concatenate([jnp.broadcast_to(y[:, j * B : (j + 1) * B], (B, B)) for j in range(chunks)], axis=0))
    parts3 = [c.astype(jnp.float32) for c in split3(down(z, linv))]
    stack = jnp.concatenate(parts3 + [jnp.zeros((5, rank), jnp.float32)], axis=0).astype(jnp.bfloat16)
    moved = lax.dot_general(stack, pan_ref[0], (((1,), (1,)), ((), ())), preferred_element_type=jnp.float32)
    moved = moved[0:1] + moved[1:2] + moved[2:3]
    result = filt_ref[...] + moved
    out_ref[...] = result

    @pl.when(has_before)
    def _():
        later[...] = result
        handoff().start()

    for j in range(chunks):
        for copy in (near(j), direct(j), relay(j), forward(j)):
            copy.wait_send()
    for g in range(len(spans)):
        exchange(g).wait_send()
        across(g).wait_send()
        arrive(parts[g].at[1:], sem_sum.at[g, 2])
        arrive(full[g].at[core, 1:], sem_sum.at[g, 4])

    @pl.when(has_before)
    def _():
        handoff().wait_send()


def spans_of(chunks):
    return [(j, j + 1) for j in range(chunks)]


def smooth(filtered, panels, tiles, neighbours, noise_var, end_smoothed):
    n, sections = lax.axis_size("cells"), lax.axis_size("tm")
    steps, cells, rank = panels.shape
    assert steps == 1 and n % 4 == 0 and B % n == 0
    chunks, chips = rank // B, n // 2
    spans = spans_of(chunks)
    f32 = jnp.float32
    vmem = pl.BlockSpec(memory_space=pltpu.VMEM)

    def sums(*lead):
        return [pltpu.VMEM((*lead, chips, (end - first) * B // n, end * B), f32) for first, end in spans]

    return pl.pallas_call(
        functools.partial(kernel, n, sections),
        out_shape=jax.ShapeDtypeStruct((steps, cells), f32),
        in_specs=[vmem, vmem, pl.BlockSpec(memory_space=pl.ANY), pl.BlockSpec(memory_space=pltpu.SMEM), vmem, vmem],
        out_specs=vmem,
        scratch_shapes=[
            pltpu.VMEM((cells, rank), f32),
            pltpu.VMEM((cells, rank), f32),
            pltpu.VMEM((5, chunks, cells, B), panels.dtype),
            pltpu.VMEM((5, steps, cells), f32),
            pltpu.VMEM(tiles.shape, tiles.dtype),
            pltpu.VMEM((cells, 5 * cells), tiles.dtype),
            pltpu.VMEM((cells, B), f32),
            pltpu.VMEM((rank, B), f32),
            pltpu.VMEM((chunks, B, rank), f32),
            pltpu.VMEM((chunks, B, rank), f32),
            pltpu.VMEM((rank, rank), f32),
            pltpu.VMEM((1, cells), f32),
            pltpu.VMEM((1, cells), f32),
            pltpu.VMEM((1, rank), f32),
            pltpu.VMEM((n, 1, rank), f32),
            pltpu.VMEM((1, cells), f32),
            pltpu.SemaphoreType.DMA,
            pltpu.SemaphoreType.DMA((2, 4, chunks)),
            pltpu.SemaphoreType.DMA((2, 5)),
            pltpu.SemaphoreType.DMA((len(spans), 8)),
            pltpu.SemaphoreType.DMA((2,)),
            pltpu.SemaphoreType.DMA((2,)),
            *sums(2), *sums(), *sums(), *sums(), *sums(2),
        ],
        compiler_params=pltpu.CompilerParams(collective_id=0, has_side_effects=True, vmem_limit_bytes=56 << 20),
    )(panels, filtered, tiles, neighbours, noise_var[None], end_smoothed[None])


def solution(mesh):
    placed = (
        P("tm", "cells"),
        P("tm", "cells", None),
        P("cells", None, None, None),
        P("cells", None),
        P("cells"),
        P("cells"),
    )
    return jax.shard_map(smooth, mesh=mesh, in_specs=placed, out_specs=P("tm", "cells"), check_vma=False)
```

```python
import functools
import jax
import jax.numpy as jnp
from jax import lax
from jax.experimental import pallas as pl
from jax.experimental.pallas import tpu as pltpu
from jax.sharding import PartitionSpec as P

HI = lax.Precision.HIGHEST
B = 128
MESH = pl.DeviceIdType.MESH
PLAN = ("B0 D0 B1 D1", "P0 R0 F0 D2", "R1 X0 F1 D3", "R2 X1 S0 F2", "R3 X2 S1 F3", "A0 A1 S2 X3", "W0 V0 W1 A2", "S3 V1 W2 A3", "V2 W3 V3")
INSIDE = {0: {}, 1: {}, 2: {1: "L1"}, 3: {1: "L2", 4: "L3"}}


def invert_block(s, n, inside_of=None):
    groups = n // 8
    inside_of = inside_of or {}
    rows = [s[8 * g : 8 * g + 8, :] for g in range(groups)]
    lane = lax.broadcasted_iota(jnp.int32, (8, n), 1)
    sub = lax.broadcasted_iota(jnp.int32, (8, n), 0)
    spread = lambda v, j: jnp.broadcast_to(v[j : j + 1, :], (8, n))
    pending = []
    for g in range(groups):
        k = 8 * g
        inside = (lane >= k) & (lane < k + 8)
        col = lambda i, j, k=k: jnp.broadcast_to(rows[i][:, k + j : k + j + 1], (8, n))
        d = [col(g, j) for j in range(8)]
        lead = jnp.where(inside, jnp.where(lane - k == sub, 1.0, 0.0), rows[g])
        each = -(-len(pending) // 8)
        for j in range(8):
            inverse = 1.0 / spread(d[j], j)
            for l in range(j + 1, 8):
                moved = spread(d[l], j) * inverse
                d[l] = jnp.where(sub == j, moved, d[l] - d[j] * moved)
            fresh = spread(lead, j) * inverse
            lead = jnp.where(sub == j, fresh, lead - d[j] * fresh)
            for _ in range(each):
                if pending:
                    pending.pop(0)()
        spreads = [spread(lead, j) for j in range(8)]

        def update(i, spreads=spreads, inside=inside, col=col):
            cols = [col(i, j) for j in range(8)]
            a = jnp.where(inside, 0.0, rows[i])
            b = cols[4] * spreads[4]
            for j in range(4):
                a = a - cols[j] * spreads[j]
            for j in range(5, 8):
                b = b + cols[j] * spreads[j]
            rows[i] = a - b

        rows[g] = lead
        if g + 1 < groups:
            update(g + 1)
        pending = [functools.partial(update, i) for i in list(range(g + 2, groups)) + list(range(g))]
        if g in inside_of:
            inside_of[g]()
    for run in pending:
        run()
    return jnp.concatenate(rows, axis=0)


def dot(a, b):
    return jnp.dot(a, b, precision=HI, preferred_element_type=jnp.float32)


def dot_t(a, b):
    return lax.dot_general(a, b, (((1,), (1,)), ((), ())), precision=HI, preferred_element_type=jnp.float32)


def down(v, ref):
    length, width = ref.shape
    spread = jnp.broadcast_to(v, (B, length))
    column = jnp.concatenate([spread[:, i : i + B].T for i in range(0, length, B)], axis=0)
    return jnp.sum(ref[...] * jnp.concatenate([column] * (width // B), axis=1), axis=0, keepdims=True)


def lanes(t):
    folded = t[:, :B]
    for i in range(B, t.shape[1], B):
        folded = folded + t[:, i : i + B]
    sums = [jnp.sum(folded[i : i + B].T, axis=0, keepdims=True) for i in range(0, t.shape[0], B)]
    return jnp.concatenate(sums, axis=1)


def split3(v):
    a = v.astype(jnp.bfloat16)
    rest = v - a.astype(jnp.float32)
    b = rest.astype(jnp.bfloat16)
    c = (rest - b.astype(jnp.float32)).astype(jnp.bfloat16)
    return a, b, c


def kernel(n, sections, pan_ref, filt_ref, tiles_ref, near_ref, noise_ref, end_ref, out_ref, adv, scaled, window, means, tiles,
           dense, divisor, q_ref, t_ref, u_ref, turned, linv, pred, later, mine, seen, passed, sem_tiles, sem_halo, sem_mean, sem_sum, sem_share,
           sem_tm, *sums):
    me = lax.axis_index("cells")
    section = lax.axis_index("tm")
    cells, rank = adv.shape
    blocks, per_row, size = tiles.shape[:3]
    chunks = rank // B
    spans = spans_of(chunks)
    packed, landed, parts, slots, full = (sums[i * len(spans) : (i + 1) * len(spans)] for i in range(5))
    chips = n // 2
    chip, core = me // 2, me % 2
    odd = chip % 2
    partner = chip * 2 + (1 - core)
    has_next = section < sections - 1
    has_before = section > 0
    is_last = section == sections - 1

    fetch = pltpu.make_async_copy(tiles_ref, tiles, sem_tiles)
    fetch.start()
    barrier = pltpu.get_barrier_semaphore()
    for k in range(1, n):
        pl.semaphore_signal(barrier, inc=1, device_id={"cells": (me + k) % n}, device_id_type=MESH)

    @pl.when(has_next)
    def _():
        pl.semaphore_signal(barrier, inc=1, device_id={"tm": section + 1}, device_id_type=MESH)

    @pl.when(has_before)
    def _():
        pl.semaphore_signal(barrier, inc=1, device_id={"tm": section - 1}, device_id_type=MESH)

    pl.semaphore_wait(barrier, n - 1 + has_next.astype(jnp.int32) + has_before.astype(jnp.int32))

    def remote(source, target, send, receive, cell):
        return pltpu.make_async_remote_copy(source, target, send, receive, device_id={"cells": cell}, device_id_type=MESH)

    def arrive(ref, sem):
        pltpu.make_async_copy(ref, ref, sem).wait()

    def mean_copy(offset):
        return remote(filt_ref, means.at[2 - offset], sem_mean.at[0, 2 - offset], sem_mean.at[1, 2 - offset], (me + offset + n) % n)

    def own_chunk(j):
        return pan_ref.at[0, :, j * B : (j + 1) * B]

    def near(j):
        return remote(own_chunk(j), window.at[1 + 2 * core, j], sem_halo.at[0, 0, j], sem_halo.at[1, 0, j], partner)

    def direct(j):
        return remote(own_chunk(j), window.at[4 * odd, j], sem_halo.at[0, 1, j], sem_halo.at[1, 1, j], me + 2 - 4 * odd)

    def relay(j):
        return remote(
            window.at[4 - 4 * odd, j], window.at[4 * odd, j], sem_halo.at[0, 2, j], sem_halo.at[1, 2, j],
            (me + 4 - 8 * odd + n) % n,
        )

    def forward(j):
        return remote(window.at[4 - 4 * core, j], window.at[3 - 2 * core, j], sem_halo.at[0, 3, j], sem_halo.at[1, 3, j], partner)

    for j in range(chunks):
        direct(j).start()
        near(j).start()
        if j == 0:
            for offset in (1, -1, 2, -2):
                mean_copy(offset).start()

    divisor[...] = jnp.broadcast_to(noise_ref[...], (B, cells)).T
    first_block = (me - 2) * blocks
    total_blocks = n * blocks

    def event_b(b):
        if b == 0:
            fetch.wait()
        places = [(near_ref[b, k] - first_block + total_blocks) % total_blocks for k in range(per_row)]
        for w in range(5 * blocks):
            at = jnp.int32(0)
            found = jnp.int32(0)
            for k in range(per_row):
                hit = (places[k] == w).astype(jnp.int32)
                at = jnp.maximum(at, hit * k)
                found = jnp.maximum(found, hit)
            keep = jnp.full((size, size), found, jnp.int32) > 0
            tile = tiles[b, at].astype(jnp.float32)
            dense[b * size : (b + 1) * size, w * size : (w + 1) * size] = jnp.where(keep, tile, 0.0).astype(jnp.bfloat16)

    def event_p(_):
        for offset in (1, -1, 2, -2):
            mean_copy(offset).wait()
        total = jnp.zeros((1, cells), jnp.float32)
        for s in range(5):
            row = filt_ref[...] if s == 2 else means[s]
            total = total + lax.dot_general(
                row.astype(jnp.bfloat16), dense[:, s * cells : (s + 1) * cells],
                (((1,), (1,)), ((), ())), preferred_element_type=jnp.float32,
            )
        pred[...] = total

    def exchange(j):
        return remote(packed[j].at[1 - core], landed[j], sem_sum.at[j, 0], sem_sum.at[j, 1], partner)

    def spread(j, k):
        q = (chip + k) % chips
        return remote(parts[j].at[q], slots[j].at[k], sem_sum.at[j, 2], sem_sum.at[j, 3], q * 2 + core)

    def collect(j, k):
        q = (chip + k) % chips
        piece = full[j].at[core, chip]
        return remote(piece, piece, sem_sum.at[j, 4], sem_sum.at[j, 5], q * 2 + core)

    def across(j):
        return remote(full[j].at[core], full[j].at[core], sem_sum.at[j, 6], sem_sum.at[j, 7], partner)

    def project():
        gap = later[...] - pred[...]
        mine[...] = down(gap, scaled)
        for k in range(1, n):
            remote(mine, seen.at[me], sem_share.at[0], sem_share.at[1], (me + k) % n).start()
        seen[me] = mine[...]

    def shared():
        arrive(seen.at[1:], sem_share.at[1])
        total = seen[0]
        for k in range(1, n):
            total = total + seen[k]
        return total

    def event_d(j):
        direct(j).wait_recv()
        relay(j).start()

        @pl.when(core == odd)
        def _():
            forward(j).start()

    def event_r(j):
        relay(j).wait_recv()

        @pl.when(core != odd)
        def _():
            forward(j).start()

    def event_f(g):
        first, end = spans[g]
        here = slice(first * B, end * B)
        for j in range(first, end):
            near(j).wait_recv()
            forward(j).wait_recv()
        product = jnp.zeros((cells, (end - first) * B), jnp.float32)
        for s in range(5):
            if s == 2:
                piece = pan_ref[0, :, here]
            else:
                piece = jnp.concatenate([window[s, j] for j in range(first, end)], axis=1)
            product = product + jnp.dot(dense[:, s * cells : (s + 1) * cells], piece, preferred_element_type=jnp.float32)
        adv[:, here] = product
        scaled[:, here] = product / jnp.concatenate([divisor[...]] * (end - first), axis=1)
        value = lax.dot_general(
            scaled[:, here], adv[:, : end * B], (((0,), (0,)), ((), ())), precision=HI, preferred_element_type=jnp.float32
        )
        per = (end - first) * B // n
        for half in range(2):
            for q in range(chips):
                at = (half * chips + q) * per
                packed[g][half, q] = value[at : at + per]
        exchange(g).start()
        if end == chunks:

            @pl.when(is_last)
            def _():
                later[...] = end_ref[...]
                project()

    def event_x(j):
        exchange(j).wait_recv()
        parts[j][...] = packed[j][core] + landed[j][...]
        for k in range(1, chips):
            spread(j, k).start()

    def event_s(j):
        arrive(slots[j].at[1:], sem_sum.at[j, 3])
        total = parts[j][chip]
        for k in range(1, chips):
            total = total + slots[j][k]
        full[j][core, chip] = total
        for k in range(1, chips):
            collect(j, k).start()

    def event_a(j):
        arrive(full[j].at[core, 1:], sem_sum.at[j, 5])
        across(j).start()

    eye = jnp.where(lax.broadcasted_iota(jnp.int32, (B, B), 0) == lax.broadcasted_iota(jnp.int32, (B, B), 1), 1.0, 0.0)

    def event_w(g):
        across(g).wait_recv()

    def block(j, i):
        g = max(at for at, span in enumerate(spans) if span[0] <= j)
        first, end = spans[g]
        value = full[g][:, :, :, i * B : (i + 1) * B].reshape((end - first) * B, B)
        return value[(j - first) * B : (j - first + 1) * B]

    def upper(j, i):
        u = block(j, i)
        if i > 0:
            u = u - dot(t_ref[j, :, : i * B], turned[i, : i * B, :])
        u_ref[j, :, i * B : (i + 1) * B] = u
        turned[j, i * B : (i + 1) * B, :] = u.T

    def times_inverse(j, i):
        here = slice(i * B, (i + 1) * B)
        t_ref[j, :, here] = dot(u_ref[j, :, here], q_ref[i * B : (i + 1) * B, :])

    def event_l(j):
        linv[j * B : (j + 1) * B, : j * B] = -dot(t_ref[j, :, : j * B], linv[: j * B, : j * B])

    def event_u(j):
        for i in range(j - 1):
            upper(j, i)
            times_inverse(j, i)
        upper(j, j - 1)
        ready.add(j)

    ready = set()

    def event_v(j):
        if j > 0 and j not in ready:
            event_u(j)
        if j > 0:
            times_inverse(j, j - 1)
        schur = block(j, j) + eye
        if j > 0:
            schur = schur - dot(t_ref[j, :, : j * B], turned[j, : j * B, :])
        linv[j * B : (j + 1) * B, j * B : (j + 1) * B] = eye
        if j + 1 < chunks:
            linv[j * B : (j + 1) * B, (j + 1) * B :] = jnp.zeros((B, rank - (j + 1) * B), jnp.float32)
        q_ref[j * B : (j + 1) * B, :] = invert_block(
            schur, B, {group: functools.partial(play, names) for group, names in INSIDE[j].items()}
        )

    events = {
        "B": event_b, "P": event_p, "D": event_d, "R": event_r, "F": event_f, "X": event_x, "S": event_s,
        "A": event_a, "W": event_w, "U": event_u, "L": event_l, "V": event_v,
    }

    def play(names):
        for name in names.split():
            events[name[0]](int(name[1:]))

    for names in PLAN:
        play(names)

    def handoff():
        return pltpu.make_async_remote_copy(
            later, passed, sem_tm.at[0], sem_tm.at[1], device_id={"tm": section - 1}, device_id_type=MESH
        )

    @pl.when(has_next)
    def _():
        handoff().wait_recv()
        later[...] = passed[...]
        project()

    g = shared()
    arrive(seen.at[1:], sem_share.at[0])
    y = lanes(linv[...] * g)
    z = lanes(q_ref[...] * jnp.concatenate([jnp.broadcast_to(y[:, j * B : (j + 1) * B], (B, B)) for j in range(chunks)], axis=0))
    parts3 = [c.astype(jnp.float32) for c in split3(down(z, linv))]
    stack = jnp.concatenate(parts3 + [jnp.zeros((5, rank), jnp.float32)], axis=0).astype(jnp.bfloat16)
    moved = lax.dot_general(stack, pan_ref[0], (((1,), (1,)), ((), ())), preferred_element_type=jnp.float32)
    moved = moved[0:1] + moved[1:2] + moved[2:3]
    result = filt_ref[...] + moved
    out_ref[...] = result

    @pl.when(has_before)
    def _():
        later[...] = result
        handoff().start()

    for j in range(chunks):
        for copy in (near(j), direct(j), relay(j), forward(j)):
            copy.wait_send()
    for g in range(len(spans)):
        exchange(g).wait_send()
        across(g).wait_send()
        arrive(parts[g].at[1:], sem_sum.at[g, 2])
        arrive(full[g].at[core, 1:], sem_sum.at[g, 4])

    @pl.when(has_before)
    def _():
        handoff().wait_send()


def spans_of(chunks):
    return [(j, j + 1) for j in range(chunks)]


def smooth(filtered, panels, tiles, neighbours, noise_var, end_smoothed):
    n, sections = lax.axis_size("cells"), lax.axis_size("tm")
    steps, cells, rank = panels.shape
    assert steps == 1 and n % 4 == 0 and B % n == 0
    chunks, chips = rank // B, n // 2
    spans = spans_of(chunks)
    f32 = jnp.float32
    vmem = pl.BlockSpec(memory_space=pltpu.VMEM)

    def sums(*lead):
        return [pltpu.VMEM((*lead, chips, (end - first) * B // n, end * B), f32) for first, end in spans]

    return pl.pallas_call(
        functools.partial(kernel, n, sections),
        out_shape=jax.ShapeDtypeStruct((steps, cells), f32),
        in_specs=[vmem, vmem, pl.BlockSpec(memory_space=pl.ANY), pl.BlockSpec(memory_space=pltpu.SMEM), vmem, vmem],
        out_specs=vmem,
        scratch_shapes=[
            pltpu.VMEM((cells, rank), f32),
            pltpu.VMEM((cells, rank), f32),
            pltpu.VMEM((5, chunks, cells, B), panels.dtype),
            pltpu.VMEM((5, steps, cells), f32),
            pltpu.VMEM(tiles.shape, tiles.dtype),
            pltpu.VMEM((cells, 5 * cells), tiles.dtype),
            pltpu.VMEM((cells, B), f32),
            pltpu.VMEM((rank, B), f32),
            pltpu.VMEM((chunks, B, rank), f32),
            pltpu.VMEM((chunks, B, rank), f32),
            pltpu.VMEM((chunks, rank, B), f32),
            pltpu.VMEM((rank, rank), f32),
            pltpu.VMEM((1, cells), f32),
            pltpu.VMEM((1, cells), f32),
            pltpu.VMEM((1, rank), f32),
            pltpu.VMEM((n, 1, rank), f32),
            pltpu.VMEM((1, cells), f32),
            pltpu.SemaphoreType.DMA,
            pltpu.SemaphoreType.DMA((2, 4, chunks)),
            pltpu.SemaphoreType.DMA((2, 5)),
            pltpu.SemaphoreType.DMA((len(spans), 8)),
            pltpu.SemaphoreType.DMA((2,)),
            pltpu.SemaphoreType.DMA((2,)),
            *sums(2), *sums(), *sums(), *sums(), *sums(2),
        ],
        compiler_params=pltpu.CompilerParams(collective_id=0, has_side_effects=True, vmem_limit_bytes=56 << 20),
    )(panels, filtered, tiles, neighbours, noise_var[None], end_smoothed[None])


def solution(mesh):
    placed = (
        P("tm", "cells"),
        P("tm", "cells", None),
        P("cells", None, None, None),
        P("cells", None),
        P("cells"),
        P("cells"),
    )
    return jax.shard_map(smooth, mesh=mesh, in_specs=placed, out_specs=P("tm", "cells"), check_vma=False)
```
